256 devices in a mesh: dp: 8 (over x, core), expert: 32 (over z, y).
Axes of the slice: x: 4, y: 4, z: 8, core: 2. Of those that a mesh axis runs over, the one named last changes fastest.
Arguments:
- out_grad: bfloat16 [32768, 2048], P(('dp', 'expert')), may hold values from -6 to 6
- combine: bfloat16 [32768, 6], P(('dp', 'expert')), may hold values from 0.049804688 to 0.59765625
- expert_ids: int32 [32768, 6], P(('dp', 'expert')), may hold values from 0 to 31, all different within a row; in each aligned block of 128 rows (0 to 127, 128 to 255, ...) at most 32 rows name the same one
- hidden: bfloat16 [32, 256, 32, 1408], P('expert', 'dp'), may hold values from -0.59765625 to 0.59765625
- w_down: bfloat16 [32, 2048, 1408], P('expert'), may hold values from -0.15625 to 0.15625
Outputs:
- grad_hidden: bfloat16 [32, 256, 32, 1408], P('expert', 'dp')
- grad_down: bfloat16 [32, 2048, 1408], P('expert', 'dp')
- grad_probs: float32 [32768, 6], P(('dp', 'expert'))
The draws below stay inside these ranges and needn't reach their ends.
Inputs may be any that keep to these rules, and one draw needn't show every extreme that they name: `expert_ids`: each row names 6 different experts. Among the 128 rows of one source device no expert is named more than 32 times, and in every draw some expert is named exactly 32 times by the rows of some device.
All inputs are finite; a program needn't handle non-finite values.
Results may differ from the reference program's by a relative error of at most 0.013.
Values may be sent and summed in bfloat16 or wider, within the bound.
A program may use at most 64 MiB of HBM per device.

```python
import math
import jax
import jax.numpy as jnp
import numpy as np
from jax import lax

D = 2048
FF = 1408
TOP = 6
TOK_DEV = 128
REPLICAS = 8
GROUP = 32
SOURCES = 256
TOKENS = 32768
EXPERTS = 32
CAP = 32


def steps_of(stream_key, dims, split, low, largest):
    def one(axis_at, shards_of):
        draws = jax.random.uniform(jax.random.fold_in(jax.random.fold_in(stream_key, 6), axis_at), (shards_of,), jnp.float32, low / len(split), largest / len(split))
        return jnp.repeat(jnp.exp(draws), dims[axis_at] // shards_of).reshape((-1,) + (1,) * (len(dims) - axis_at - 1))

    level = one(*split[0])
    for cut in split[1:]:
        level = level * one(*cut)
    return level


def deal_out(stream_key, own, number, rows, count, top, most, slope):
    sequence = jax.random.permutation(stream_key, count)
    crowded, usual = shares(count, rows * top, most, slope, True), shares(count, rows * top, most, slope, False)
    places = jnp.arange(count)

    def named(lengths, turn):
        used = int((lengths > 0).sum())
        fixed = max(1, used // 4)
        moved = fixed + (places - fixed + turn * (used - fixed)) % max(1, count - fixed)
        return jnp.zeros((count,), jnp.int32).at[sequence[jnp.where(places < fixed, places, moved)]].set(jnp.asarray(lengths, jnp.int32))

    lengths = jnp.where(number % 4 == 0, named(crowded, number // 4), named(usual, number - number // 4 - 1))
    mixed = jax.random.permutation(jax.random.fold_in(own, 3), count)
    donor, taker = mixed[0:count // 2 * 2:2], mixed[1:count // 2 * 2:2]
    room = jnp.minimum(lengths[donor] - 1, most - lengths[taker]) // 2
    room = jnp.where((donor == sequence[0]) | (taker == sequence[0]) | (lengths[taker] == 0), 0, jnp.maximum(room, 0))
    moved = jax.random.randint(jax.random.fold_in(own, 4), (count // 2,), 0, 1 << 20) % (room + 1)
    lengths = lengths.at[donor].add(-moved).at[taker].add(moved)
    items = jnp.searchsorted(jnp.cumsum(lengths), jnp.arange(rows * top), side="right").astype(jnp.int32)
    listing = items.reshape(top, rows).T
    listing = listing[jax.random.permutation(jax.random.fold_in(own, 1), rows)]
    turn = jax.random.randint(jax.random.fold_in(own, 2), (rows, 1), 0, top)
    return jnp.take_along_axis(listing, (jnp.arange(top)[None, :] + turn) % top, axis=1)


def shares(count, total, limit, lean, full):
    loads = [(1 << 20) // math.isqrt(grade ** lean) + 1 for grade in range(1, count + 1)]
    largest = limit if full else min(limit, max(-(-total // count), total * loads[0] // sum(loads)))
    least = 1 if total - largest >= count - 1 else 0
    given, surplus = [largest] + [least] * (count - 1), total - largest - least * (count - 1)
    while surplus > 0:
        movable = [i for i in range(1, count) if given[i] < largest] or [i for i in range(1, count) if given[i] < limit]
        whole, left = sum([loads[i] for i in movable]), surplus
        for i in movable:
            more = min(limit - given[i], max(1, left * loads[i] // whole), surplus)
            given[i] = given[i] + more
            surplus = surplus - more
    return np.array(given)


def gaussian(rng, extent, scale, bound, cuts=(), kind=jnp.bfloat16):
    array = scale * jax.random.normal(rng, extent, jnp.float32)
    if cuts:
        array = array * steps_of(rng, extent, cuts, -0.22, 0.18)
    return jnp.clip(array, -bound, bound).astype(kind)


def setup_inputs(seed: int = 0) -> dict:
    key_list = jax.random.split(jax.random.key(seed), 6)
    out_grad = gaussian(key_list[0], (TOKENS, D), 1.0, 6.0, ((0, 256),))
    combine = jnp.clip(jnp.exp(math.log(0.59765625) - 2.4849066 * jax.random.uniform(key_list[1], (TOKENS, TOP), jnp.float32) ** steps_of(key_list[1], (TOKENS, TOP), ((0, 256),), -0.2, 0.2)), 0.049804688, 0.59765625).astype(jnp.bfloat16)
    expert_ids_keys = jax.random.split(jax.random.fold_in(key_list[2], 1), TOKENS // TOK_DEV)
    expert_ids_turns = jax.random.permutation(jax.random.fold_in(key_list[2], 3), TOKENS // TOK_DEV)
    expert_ids = jax.vmap(lambda own, number: deal_out(jax.random.fold_in(key_list[2], 2), own, number, TOK_DEV, EXPERTS, TOP, CAP, 2))(expert_ids_keys, expert_ids_turns).reshape((TOKENS, TOP))
    hidden = gaussian(key_list[3], (EXPERTS, SOURCES, CAP, FF), 0.1, 0.59765625, ((0, 32), (1, 8)))
    w_down = gaussian(key_list[4], (EXPERTS, D, FF), FF ** -0.5, 0.15625, ((0, 32),))
    return {"out_grad": out_grad, "combine": combine, "expert_ids": expert_ids, "hidden": hidden, "w_down": w_down}


def reference(out_grad, combine, expert_ids, hidden, w_down):
    pair_total = TOKENS * TOP
    chosen_grid = expert_ids.reshape(SOURCES, TOK_DEV * TOP)
    onehot = (chosen_grid[:, :, None] == jnp.arange(EXPERTS, dtype=jnp.int32)[None, None, :]).astype(jnp.int32)
    before = jnp.cumsum(onehot, axis=1) - onehot
    slot_rank = jnp.sum(before * onehot, axis=2).reshape(-1).astype(jnp.int32)
    source = (jnp.arange(pair_total, dtype=jnp.int32) // (TOK_DEV * TOP)).astype(jnp.int32)
    chosen = expert_ids.reshape(-1).astype(jnp.int32)
    bucket_pos = ((chosen * SOURCES + source) * CAP + slot_rank).astype(jnp.int32)
    pair_of = jnp.full((EXPERTS * SOURCES * CAP,), pair_total, jnp.int32)
    pair_of = pair_of.at[bucket_pos].set(jnp.arange(pair_total, dtype=jnp.int32))
    token_of = jnp.where(pair_of < pair_total, pair_of // TOP, TOKENS).astype(jnp.int32)
    grad_rows = jnp.concatenate([out_grad, jnp.zeros((1, D), out_grad.dtype)], axis=0)
    prob_rows = jnp.concatenate([combine.reshape(-1), jnp.zeros((1,), combine.dtype)], axis=0)
    token_table = token_of.reshape(EXPERTS, SOURCES * CAP)
    pair_table = pair_of.reshape(EXPERTS, SOURCES * CAP)

    def per_expert(packed):
        token_idx, pair_idx, saved, weight = packed
        slot_rows = grad_rows[token_idx]
        slot_prob = prob_rows[pair_idx].astype(jnp.float32)[:, None]
        saved_rows = saved.reshape(SOURCES * CAP, FF)
        projected = jnp.dot(slot_rows, weight, preferred_element_type=jnp.float32)
        hidden_grad = (slot_prob * projected).astype(jnp.bfloat16)
        slot_grad = jnp.sum(projected * saved_rows.astype(jnp.float32), axis=1)
        scaled = (slot_prob * slot_rows.astype(jnp.float32)).astype(jnp.bfloat16)
        partial_value = jnp.einsum("rnd,rnf->rdf",
                             scaled.reshape(REPLICAS, GROUP * CAP, D).astype(jnp.float32),
                             saved_rows.reshape(REPLICAS, GROUP * CAP, FF).astype(jnp.float32))
        partial_value = lax.optimization_barrier(partial_value.astype(jnp.bfloat16))
        down_grad = jnp.sum(partial_value.astype(jnp.float32), axis=0).astype(jnp.bfloat16)
        return hidden_grad.reshape(SOURCES, CAP, FF), slot_grad, down_grad

    grad_hidden, slot_grads, grad_down = lax.map(per_expert, (token_table, pair_table, hidden, w_down))
    grad_probs = slot_grads.reshape(-1)[bucket_pos].reshape(TOKENS, TOP)
    return grad_hidden, grad_down, grad_probs
```

```python
import functools

import jax
import jax.numpy as jnp
from jax import lax
from jax.experimental import pallas as pl
from jax.experimental.pallas import tpu as pltpu
from jax.sharding import PartitionSpec as P

MESH = pl.DeviceIdType.MESH
F32 = jnp.float32
BF16 = jnp.bfloat16
X, Y, Z = 4, 4, 8
PHASES = 2
RELAY_LAG = 2
ARRIVE_LAG = 4


def column_chunks(width):
    step = 512
    return [(at, min(step, width - at)) for at in range(0, width, step)]


def kernel(
    tok, ids, comb, hid_in, w_in, gh, gd, gp,
    own, zbuf, tab, pick, sel, relay, rows, prow, hid, phid, wv, acc, ghb,
    sums, send2, direct, relayed, relay_in, final_in, gdb, sg, sgy, sgu, sgz,
    sems,
):
    tokens, group_cols = own.shape[1:]
    sub = group_cols // X
    cap = tokens // Y
    inner = hid.shape[-1]
    chunks = column_chunks(inner)
    dp, ex = lax.axis_index("dp"), lax.axis_index("expert")
    x, core = dp // 2, dp % 2
    z, y = ex // Y, ex % Y
    y_a, y_b, y_far = y + 1 - 2 * (y % 2), Y - 1 - y, (y + 2) % Y

    def at_ex(zz, yy):
        return {"expert": zz * Y + yy}

    def at_dp(xx, cc):
        return {"dp": xx * 2 + cc}

    up, down = at_ex((z + 1) % Z, y), at_ex((z + Z - 1) % Z, y)
    side_a, side_b, side_far = at_ex(z, y_a), at_ex(z, y_b), at_ex(z, y_far)
    right, left = at_dp((x + 1) % X, core), at_dp((x + X - 1) % X, core)
    partner = at_dp(x, 1 - core)

    taken = [0]
    started = []

    def sem():
        taken[0] += 1
        return sems.at[taken[0] - 1]

    def local(src, dst):
        copy = pltpu.make_async_copy(src, dst, sem())
        copy.start()
        return copy

    def remote(src, dst, device):
        copy = pltpu.make_async_remote_copy(
            src_ref=src, dst_ref=dst, send_sem=sem(), recv_sem=sem(),
            device_id=device, device_id_type=MESH,
        )
        copy.start()
        started.append(copy)
        return copy

    own_loads = []
    for g in range(2 * PHASES):
        ph, cc = g // 2, g % 2
        own_loads.append([
            local(tok.at[:, pl.ds(q * 2 * 256 + cc * 256 + ph * sub, sub)],
                  own.at[g, :, pl.ds(q * sub, sub)])
            for q in range(X)
        ])
    hid_load = local(hid_in, hid)
    w_loads = []
    for ph in range(PHASES):
        for cc in range(2):
            for q in range(X):
                w_loads.append(local(
                    w_in.at[pl.ds(q * 512 + cc * 256 + ph * sub, sub)],
                    wv.at[ph, pl.ds(cc * group_cols + q * sub, sub)]))

    barrier = pltpu.get_barrier_semaphore()
    peers = [at_ex((z + d) % Z, y) for d in range(1, Z)]
    peers += [side_a, side_b, side_far, right, left, partner]
    for peer in peers:
        pl.semaphore_signal(barrier, inc=1, device_id=peer, device_id_type=MESH)

    ids_f = ids[...].astype(F32)
    comb_f = comb[...].astype(F32)
    picks = ids_f.shape[0]
    pad = 8 - picks
    tab[0] = jnp.concatenate([
        ids_f, jnp.full((pad, tokens), -1.0, F32), comb_f, jnp.zeros((pad, tokens), F32)
    ], axis=0).astype(BF16)
    before = (
        lax.broadcasted_iota(jnp.int32, (tokens, tokens), 0)
        < lax.broadcasted_iota(jnp.int32, (tokens, tokens), 1)
    ).astype(F32).astype(BF16)
    slot_of_row = lax.broadcasted_iota(jnp.int32, (cap, tokens), 0).astype(F32)

    def make_pick(si):
        table = tab[si].astype(F32)
        named, weight = table[0:8], table[8:16]
        chosen, probs = [], []
        for yy in (y_a, y_far, y_b, y):
            hit = named == (z * Y + yy).astype(F32)
            chosen.append(jnp.sum(jnp.where(hit, 1.0, 0.0), axis=0, keepdims=True))
            probs.append(jnp.sum(jnp.where(hit, weight, 0.0), axis=0, keepdims=True))
        marks = jnp.concatenate(chosen + [jnp.zeros((4, tokens), F32)], axis=0)
        rank = jnp.dot(marks.astype(BF16), before, preferred_element_type=F32)
        blocks = []
        for b in range(4):
            slot = jnp.where(chosen[b] > 0.5, rank[b:b + 1], -1.0)
            blocks.append(jnp.where(slot_of_row == slot, probs[b], 0.0))
        pick[si] = jnp.concatenate(blocks, axis=0).astype(BF16)

    make_pick(0)
    for load in own_loads[0] + own_loads[1]:
        load.wait()
    pl.semaphore_wait(barrier, len(peers))

    def source_z(si):
        return (z + (Z - si if si < 5 else si - 4)) % Z

    z_copies, tab_copies = {}, {}

    def token_block(direction, d, g):
        return own.at[g] if d == 0 else zbuf.at[direction, d - 1, g]

    def forward(direction, d, g):
        z_copies[direction, d + 1, g] = remote(
            token_block(direction, d, g), zbuf.at[direction, d, g], (up, down)[direction])

    def tab_index(direction, d):
        return 0 if d == 0 else d + 4 * direction

    def forward_tab(direction, d):
        tab_copies[direction, d + 1] = remote(
            tab.at[tab_index(direction, d)], tab.at[tab_index(direction, d + 1)],
            (up, down)[direction])

    y_copies, relay_copies, events = {}, {}, {}

    def unit(ph, ev, g, src, si):
        u = 2 * ev + len(events.setdefault(ev, []))
        zs = source_z(si)
        block = jnp.dot(pick[si], src[...], preferred_element_type=F32).astype(BF16)
        for b in range(3):
            sel[u, b] = block[b * cap:(b + 1) * cap]
        mine = pl.ds(pl.multiple_of(y * cap, cap), cap)
        rows[g, zs, mine] = block[3 * cap:]
        relay_copies[u] = remote(sel.at[u, 1], relay.at[u], side_a)
        y_copies.setdefault((ph, si), []).extend([
            remote(sel.at[u, 0], rows.at[g, zs, mine], side_a),
            remote(sel.at[u, 2], rows.at[g, zs, mine], side_b),
        ])
        events[ev].append((ph, u, g, si, zs))

    def pass_relays(ev):
        theirs = pl.ds(pl.multiple_of(y_a * cap, cap), cap)
        for ph, u, g, si, zs in events[ev]:
            relay_copies[u].wait_recv()
            y_copies[ph, si].append(remote(relay.at[u], rows.at[g, zs, theirs], side_b))

    prow_copies = {}

    def arrive(ph, sis):
        for si in sis:
            for copy in y_copies[ph, si]:
                copy.wait_recv()
            zs = source_z(si)
            prow_copies[ph, si] = remote(
                rows.at[2 * ph + 1 - core, zs], prow.at[ph, zs], partner)

    eye = (
        lax.broadcasted_iota(jnp.int32, (tokens, tokens), 0)
        == lax.broadcasted_iota(jnp.int32, (tokens, tokens), 1)
    )
    gh_copies = []
    w_waited = [False]

    def project(ph, sis):
        if not w_waited[0]:
            w_waited[0] = True
            hid_load.wait()
            for load in w_loads:
                load.wait()
        places = [source_z(si) for si in sis]
        halves = [
            jnp.concatenate([rows[2 * ph + cc, zs] for zs in places], axis=0) for cc in range(2)
        ]
        totals = [jnp.zeros((tokens, 1), F32) for _ in sis]
        for at, width in chunks:
            cols = pl.ds(at, width)
            value = jnp.dot(
                halves[0], wv[ph, 0:group_cols, cols], preferred_element_type=F32
            ) + jnp.dot(
                halves[1], wv[ph, group_cols:2 * group_cols, cols], preferred_element_type=F32)
            for n, zs in enumerate(places):
                part = value[n * tokens:(n + 1) * tokens]
                if ph > 0:
                    part = part + acc[zs, :, cols]
                if ph < PHASES - 1:
                    acc[zs, :, cols] = part
                else:
                    ghb[zs, :, cols] = part.astype(BF16)
                    totals[n] = totals[n] + jnp.sum(
                        part * hid[zs, :, cols].astype(F32), axis=1, keepdims=True)
        if ph == PHASES - 1:
            for n, zs in enumerate(places):
                gh_copies.append(local(ghb.at[zs], gh.at[zs]))
                sg[pl.ds(zs, 1), :] = jnp.sum(
                    jnp.where(eye, totals[n], 0.0), axis=0, keepdims=True)

    slices = [(x + 2) % X, (x + 1) % X, (x + X - 1) % X, x]
    half = sub // 2
    relay_sums, final_sums = {}, {}

    def weight_grad(ph, pair):
        lanes = [pl.ds(pl.multiple_of(q * sub, sub), sub) for q in slices[2 * pair:2 * pair + 2]]
        flat = Z * tokens
        mine = jnp.concatenate(
            [rows[2 * ph + core, :, :, q].reshape(flat, sub) for q in lanes], axis=1)
        others = jnp.concatenate(
            [prow[ph, :, :, q].reshape(flat, sub) for q in lanes], axis=1)
        contract = (((0,), (0,)), ((), ()))
        for at, width in chunks:
            cols = pl.ds(at, width)
            value = lax.dot_general(
                mine, hid[:, :, cols].reshape(flat, width), contract, preferred_element_type=F32
            ) + lax.dot_general(
                others, phid[:, :, cols].reshape(flat, width), contract,
                preferred_element_type=F32)
            first, second = value[0:sub], value[sub:2 * sub]
            if pair == 0:
                send2[ph, :, cols] = first.astype(BF16)
                direct[ph, 0, :, cols] = second[half:].astype(BF16)
                sums[ph, 0, :, cols] = second[0:half]
            else:
                direct[ph, 1, :, cols] = first[0:half].astype(BF16)
                sums[ph, 1, :, cols] = first[half:]
                sums[ph, 2, :, cols] = second[0:half]
                sums[ph, 3, :, cols] = second[half:]
        if pair == 0:
            relay_sums[ph] = [
                remote(send2.at[ph, pl.ds(0, half)], relay_in.at[ph, 0], right),
                remote(send2.at[ph, pl.ds(half, half)], relay_in.at[ph, 1], left),
            ]
            final_sums[ph] = [remote(direct.at[ph, 0], final_in.at[ph, 0, 1], right)]
        else:
            final_sums[ph].append(remote(direct.at[ph, 1], final_in.at[ph, 1, 0], left))

    def wait_partner(ph):
        if ph == 0:
            phid_copy.wait_recv()
        for si in range(Z):
            prow_copies[ph, si].wait_recv()

    def pass_sums(ph):
        for side in range(2):
            relay_sums[ph][side].wait_recv()
            relayed[ph, side] = (sums[ph, side] + relay_in[ph, side].astype(F32)).astype(BF16)
            final_sums[ph].append(
                remote(relayed.at[ph, side], final_in.at[ph, side, side], (right, left)[side]))

    gd_copies = []

    def finish_sums(ph):
        for copy in final_sums[ph]:
            copy.wait_recv()
        for part in range(2):
            gdb[ph, pl.ds(part * half, half)] = (
                sums[ph, 2 + part] + final_in[ph, 0, part].astype(F32)
                + final_in[ph, 1, part].astype(F32)
            ).astype(BF16)
        gd_copies.append(local(gdb.at[ph], gd.at[pl.ds(ph * sub, sub)]))

    for direction in range(2):
        forward_tab(direction, 0)
    for g in range(2):
        for direction in range(2):
            forward(direction, 0, g)
    phid_copy = remote(hid_in, phid, partner)

    arrivals = []
    for ph in range(PHASES):
        arrivals += [(8 * ph, ph, (0,))]
        arrivals += [(8 * ph + 2 * d, ph, (d, 4 + d)) for d in (1, 2, 3)]
        arrivals += [(8 * ph + 7, ph, (4,))]
    todo = {}
    for ev, ph, sis in arrivals:
        todo.setdefault(ev + ARRIVE_LAG, []).append((ph, sis))
    last = 8 * PHASES - 1

    for ev in range(8 * PHASES):
        ph, i = ev // 8, ev % 8
        g0 = 2 * ph
        if i == 0:
            unit(ph, ev, g0, own.at[g0], 0)
            unit(ph, ev, g0 + 1, own.at[g0 + 1], 0)
        elif i < 7:
            d, cc = (i + 1) // 2, (i + 1) % 2
            g = g0 + cc
            if ph == 0 and cc == 0:
                for direction in range(2):
                    tab_copies[direction, d].wait_recv()
                    if d < 4 - direction:
                        forward_tab(direction, d)
            for direction in range(2):
                z_copies[direction, d, g].wait_recv()
                if d < 3 or cc == direction:
                    forward(direction, d, g)
            if i in (5, 6) and ph + 1 < PHASES:
                for load in own_loads[g + 2]:
                    load.wait()
                for direction in range(2):
                    forward(direction, 0, g + 2)
            for direction in range(2):
                si = tab_index(direction, d)
                if ph == 0 and cc == 0:
                    make_pick(si)
                unit(ph, ev, g, zbuf.at[direction, d - 1, g], si)
        else:
            if ph == 0:
                tab_copies[0, 4].wait_recv()
                make_pick(4)
            for direction in range(2):
                z_copies[direction, 4, g0 + direction].wait_recv()
                unit(ph, ev, g0 + direction, zbuf.at[direction, 3, g0 + direction], 4)
        if ev >= RELAY_LAG:
            pass_relays(ev - RELAY_LAG)
        for ready_ph, sis in todo.pop(ev, []):
            arrive(ready_ph, sis)
            project(ready_ph, sis)
        if ph > 0 and i == 4:
            wait_partner(ph - 1)
            weight_grad(ph - 1, 0)
        if ph > 0 and i == 5:
            weight_grad(ph - 1, 1)
        if ph > 0 and i == 7:
            pass_sums(ph - 1)

    for ev in range(last - RELAY_LAG + 1, last + 1):
        pass_relays(ev)
    rest = [item for ev in sorted(todo) for item in todo[ev]]
    for ready_ph, sis in rest:
        arrive(ready_ph, sis)
    for ready_ph, sis in rest[:-1]:
        project(ready_ph, sis)
    wait_partner(PHASES - 1)
    weight_grad(PHASES - 1, 0)
    weight_grad(PHASES - 1, 1)
    project(*rest[-1])

    sgy[y] = sg[...]
    back = [remote(sg, sgy.at[y], peer) for peer in (side_a, side_b, side_far)]
    finish_sums(0)
    pass_sums(PHASES - 1)
    for copy in back:
        copy.wait_recv()
    for zz in range(Z):
        for yy in range(Y):
            sgu[zz, yy:yy + 1] = sgy[yy, zz:zz + 1]
        sgu[zz, Y:8] = jnp.zeros((8 - Y, tokens), F32)
    sgz[z] = sgu[z]
    back = [remote(sgu.at[(z + d) % Z], sgz.at[z], at_ex((z + d) % Z, y)) for d in range(1, Z)]

    row_id = lax.broadcasted_iota(jnp.int32, (8 * Z, tokens), 0)
    expert_of_row = jnp.where(row_id % 8 < Y, row_id // 8 * Y + row_id % 8, -1).astype(F32)
    marks = jnp.zeros((8 * Z, tokens), F32)
    for k in range(picks):
        marks = marks + jnp.where(expert_of_row == ids_f[k:k + 1], 1.0, 0.0)
    rank = jnp.dot(marks.astype(BF16), before, preferred_element_type=F32)
    slot = jnp.where(marks > 0.5, rank, -1.0)
    for copy in back:
        copy.wait_recv()
    table = sgz[...].reshape(8 * Z, tokens)
    values = jnp.zeros((8 * Z, cap), F32)
    for yy in range(Y):
        values = jnp.where(y == yy, table[:, yy * cap:(yy + 1) * cap], values)
    found = jnp.zeros((8 * Z, tokens), F32)
    for cc in range(cap):
        found = jnp.where(slot == float(cc), values[:, cc:cc + 1], found)
    for k in range(picks):
        gp[k:k + 1, :] = jnp.sum(
            jnp.where(expert_of_row == ids_f[k:k + 1], found, 0.0), axis=0, keepdims=True
        ) / comb_f[k:k + 1]

    finish_sums(PHASES - 1)
    for copy in started:
        copy.wait_send()
    for copy in gh_copies + gd_copies:
        copy.wait()


def body(out_grad, combine, expert_ids, hidden, w_down):
    tokens, picks = expert_ids.shape
    width = out_grad.shape[1]
    cap, inner = hidden.shape[2], hidden.shape[3]
    groups = 2 * PHASES
    gcols = width // groups
    sub = gcols // X
    flat = (Z, Y * cap)
    vmem = lambda shape, kind=BF16: pltpu.VMEM(shape, kind)
    anywhere = pl.BlockSpec(memory_space=pl.ANY)
    in_vmem = pl.BlockSpec(memory_space=pltpu.VMEM)
    grad_hidden, grad_down, grad_probs = pl.pallas_call(
        kernel,
        out_shape=(
            jax.ShapeDtypeStruct(flat + (inner,), BF16),
            jax.ShapeDtypeStruct((PHASES * sub, inner), BF16),
            jax.ShapeDtypeStruct((picks, tokens), F32),
        ),
        in_specs=[anywhere, in_vmem, in_vmem, anywhere, anywhere],
        out_specs=(anywhere, anywhere, in_vmem),
        scratch_shapes=[
            vmem((groups, tokens, gcols)),
            vmem((2, 4, groups, tokens, gcols)),
            vmem((Z, 16, tokens)),
            vmem((Z, tokens, tokens)),
            vmem((16 * PHASES, 3, cap, gcols)),
            vmem((16 * PHASES, cap, gcols)),
            vmem((groups,) + flat + (gcols,)),
            vmem((PHASES,) + flat + (gcols,)),
            vmem(flat + (inner,)),
            vmem(flat + (inner,)),
            vmem((PHASES, 2 * gcols, inner)),
            vmem(flat + (inner,), F32),
            vmem(flat + (inner,)),
            vmem((PHASES, 4, sub // 2, inner), F32),
            vmem((PHASES, sub, inner)),
            vmem((PHASES, 2, sub // 2, inner)),
            vmem((PHASES, 2, sub // 2, inner)),
            vmem((PHASES, 2, sub // 2, inner)),
            vmem((PHASES, 2, 2, sub // 2, inner)),
            vmem((PHASES, sub, inner)),
            vmem((Z, tokens), F32),
            vmem((Y, Z, tokens), F32),
            vmem((Z, 8, tokens), F32),
            vmem((Z, 8, tokens), F32),
            pltpu.SemaphoreType.DMA((512,)),
        ],
        compiler_params=pltpu.CompilerParams(
            collective_id=0, has_side_effects=True, vmem_limit_bytes=60 * 2**20),
    )(
        out_grad, expert_ids.T, combine.T,
        hidden.reshape(flat + (inner,)), w_down[0],
    )
    return (
        grad_hidden.reshape(hidden.shape),
        grad_down[None],
        grad_probs.T,
    )


def solution(mesh):
    in_specs = (
        P(("dp", "expert"), None),
        P(("dp", "expert"), None),
        P(("dp", "expert"), None),
        P("expert", "dp", None, None),
        P("expert", None, None),
    )
    out_specs = (P("expert", "dp", None, None), P("expert", "dp", None), P(("dp", "expert"), None))
    return jax.shard_map(body, mesh=mesh, in_specs=in_specs, out_specs=out_specs, check_vma=False)
```

```python
import functools

import jax
import jax.numpy as jnp
from jax import lax
from jax.experimental import pallas as pl
from jax.experimental.pallas import tpu as pltpu
from jax.sharding import PartitionSpec as P

MESH = pl.DeviceIdType.MESH
F32 = jnp.float32
BF16 = jnp.bfloat16
X, Y, Z = 4, 4, 8
PHASES = 2
ARRIVE_LAG = 2


def column_chunks(width):
    step = 512
    return [(at, min(step, width - at)) for at in range(0, width, step)]


def kernel(
    tok, ids, comb, hid_in, w_in, gh, gd, gp,
    own, zbuf, tab, pick, sel, rows, prow, hid, phid, wv, acc, ghb,
    sums, send2, direct, relayed, relay_in, final_in, gdb, sg, sgy, sgu, sgz,
    sems,
):
    tokens, group_cols = own.shape[1:]
    sub = group_cols // X
    cap = tokens // Y
    inner = hid.shape[-1]
    chunks = column_chunks(inner)
    dp, ex = lax.axis_index("dp"), lax.axis_index("expert")
    x, core = dp // 2, dp % 2
    z, y = ex // Y, ex % Y
    y_a, y_b, y_far = y + 1 - 2 * (y % 2), Y - 1 - y, (y + 2) % Y

    def at_ex(zz, yy):
        return {"expert": zz * Y + yy}

    def at_dp(xx, cc):
        return {"dp": xx * 2 + cc}

    up, down = at_ex((z + 1) % Z, y), at_ex((z + Z - 1) % Z, y)
    side_a, side_b, side_far = at_ex(z, y_a), at_ex(z, y_b), at_ex(z, y_far)
    right, left = at_dp((x + 1) % X, core), at_dp((x + X - 1) % X, core)
    partner = at_dp(x, 1 - core)

    taken = [0]
    started = []

    def sem():
        taken[0] += 1
        return sems.at[taken[0] - 1]

    def local(src, dst):
        copy = pltpu.make_async_copy(src, dst, sem())
        copy.start()
        return copy

    def remote(src, dst, device):
        copy = pltpu.make_async_remote_copy(
            src_ref=src, dst_ref=dst, send_sem=sem(), recv_sem=sem(),
            device_id=device, device_id_type=MESH,
        )
        copy.start()
        started.append(copy)
        return copy

    own_loads = []
    for g in range(2 * PHASES):
        ph, cc = g // 2, g % 2
        own_loads.append([
            local(tok.at[:, pl.ds(q * 2 * 256 + cc * 256 + ph * sub, sub)],
                  own.at[g, :, pl.ds(q * sub, sub)])
            for q in range(X)
        ])
    hid_load = local(hid_in, hid)
    w_loads = []
    for ph in range(PHASES):
        for cc in range(2):
            for q in range(X):
                w_loads.append(local(
                    w_in.at[pl.ds(q * 512 + cc * 256 + ph * sub, sub)],
                    wv.at[ph, pl.ds(cc * group_cols + q * sub, sub)]))

    barrier = pltpu.get_barrier_semaphore()
    peers = [up, down, side_a, side_b, side_far, right, left, partner]
    for peer in peers:
        pl.semaphore_signal(barrier, inc=1, device_id=peer, device_id_type=MESH)

    ids_f = ids[...].astype(F32)
    comb_f = comb[...].astype(F32)
    picks = ids_f.shape[0]
    pad = 8 - picks
    tab[0] = jnp.concatenate([
        ids_f, jnp.full((pad, tokens), -1.0, F32), comb_f, jnp.zeros((pad, tokens), F32)
    ], axis=0).astype(BF16)
    before = (
        lax.broadcasted_iota(jnp.int32, (tokens, tokens), 0)
        < lax.broadcasted_iota(jnp.int32, (tokens, tokens), 1)
    ).astype(F32).astype(BF16)
    slot_of_row = lax.broadcasted_iota(jnp.int32, (cap, tokens), 0).astype(F32)

    def make_pick(si):
        table = tab[si].astype(F32)
        named, weight = table[0:8], table[8:16]
        chosen, probs = [], []
        for yy in (y_a, y_far, y_b, y):
            hit = named == (z * Y + yy).astype(F32)
            chosen.append(jnp.sum(jnp.where(hit, 1.0, 0.0), axis=0, keepdims=True))
            probs.append(jnp.sum(jnp.where(hit, weight, 0.0), axis=0, keepdims=True))
        marks = jnp.concatenate(chosen + [jnp.zeros((4, tokens), F32)], axis=0)
        rank = jnp.dot(marks.astype(BF16), before, preferred_element_type=F32)
        blocks = []
        for b in range(4):
            slot = jnp.where(chosen[b] > 0.5, rank[b:b + 1], -1.0)
            blocks.append(jnp.where(slot_of_row == slot, probs[b], 0.0))
        pick[si] = jnp.concatenate(blocks, axis=0).astype(BF16)

    make_pick(0)
    for load in own_loads[0] + own_loads[1]:
        load.wait()
    pl.semaphore_wait(barrier, len(peers))

    def source_z(si):
        return (z + (Z - si if si < 5 else si - 4)) % Z

    z_copies, tab_copies = {}, {}

    def token_block(direction, d, g):
        return own.at[g] if d == 0 else zbuf.at[direction, d - 1, g]

    def forward(direction, d, g):
        z_copies[direction, d + 1, g] = remote(
            token_block(direction, d, g), zbuf.at[direction, d, g], (up, down)[direction])

    def tab_index(direction, d):
        return 0 if d == 0 else d + 4 * direction

    def forward_tab(direction, d):
        tab_copies[direction, d + 1] = remote(
            tab.at[tab_index(direction, d)], tab.at[tab_index(direction, d + 1)],
            (up, down)[direction])

    y_copies, events = {}, {}

    def unit(ph, ev, g, src, si):
        u = 2 * ev + len(events.setdefault(ev, []))
        zs = source_z(si)
        block = jnp.dot(pick[si], src[...], preferred_element_type=F32).astype(BF16)
        for b in range(3):
            sel[u, b] = block[b * cap:(b + 1) * cap]
        mine = pl.ds(pl.multiple_of(y * cap, cap), cap)
        rows[g, zs, mine] = block[3 * cap:]
        y_copies.setdefault((ph, si), []).extend([
            remote(sel.at[u, b], rows.at[g, zs, mine], peer)
            for b, peer in ((1, side_far), (0, side_a), (2, side_b))
        ])
        events[ev].append(u)

    prow_copies = {}

    def arrive(ph, sis):
        for si in sis:
            for copy in y_copies[ph, si]:
                copy.wait_recv()
            zs = source_z(si)
            prow_copies[ph, si] = remote(
                rows.at[2 * ph + 1 - core, zs], prow.at[ph, zs], partner)

    eye = (
        lax.broadcasted_iota(jnp.int32, (tokens, tokens), 0)
        == lax.broadcasted_iota(jnp.int32, (tokens, tokens), 1)
    )
    gh_copies = []
    w_waited = [False]

    def project(ph, sis):
        if not w_waited[0]:
            w_waited[0] = True
            hid_load.wait()
            for load in w_loads:
                load.wait()
        places = [source_z(si) for si in sis]
        halves = [
            jnp.concatenate([rows[2 * ph + cc, zs] for zs in places], axis=0) for cc in range(2)
        ]
        totals = [jnp.zeros((tokens, 1), F32) for _ in sis]
        for at, width in chunks:
            cols = pl.ds(at, width)
            value = jnp.dot(
                halves[0], wv[ph, 0:group_cols, cols], preferred_element_type=F32
            ) + jnp.dot(
                halves[1], wv[ph, group_cols:2 * group_cols, cols], preferred_element_type=F32)
            for n, zs in enumerate(places):
                part = value[n * tokens:(n + 1) * tokens]
                if ph > 0:
                    part = part + acc[zs, :, cols]
                if ph < PHASES - 1:
                    acc[zs, :, cols] = part
                else:
                    ghb[zs, :, cols] = part.astype(BF16)
                    totals[n] = totals[n] + jnp.sum(
                        part * hid[zs, :, cols].astype(F32), axis=1, keepdims=True)
        if ph == PHASES - 1:
            for n, zs in enumerate(places):
                gh_copies.append(local(ghb.at[zs], gh.at[zs]))
                sg[pl.ds(zs, 1), :] = jnp.sum(
                    jnp.where(eye, totals[n], 0.0), axis=0, keepdims=True)

    slices = [(x + 2) % X, (x + 1) % X, (x + X - 1) % X, x]
    half = sub // 2
    relay_sums, final_sums = {}, {}

    def weight_grad(ph, pair):
        lanes = [pl.ds(pl.multiple_of(q * sub, sub), sub) for q in slices[2 * pair:2 * pair + 2]]
        flat = Z * tokens
        mine = jnp.concatenate(
            [rows[2 * ph + core, :, :, q].reshape(flat, sub) for q in lanes], axis=1)
        others = jnp.concatenate(
            [prow[ph, :, :, q].reshape(flat, sub) for q in lanes], axis=1)
        contract = (((0,), (0,)), ((), ()))
        for at, width in chunks:
            cols = pl.ds(at, width)
            value = lax.dot_general(
                mine, hid[:, :, cols].reshape(flat, width), contract, preferred_element_type=F32
            ) + lax.dot_general(
                others, phid[:, :, cols].reshape(flat, width), contract,
                preferred_element_type=F32)
            first, second = value[0:sub], value[sub:2 * sub]
            if pair == 0:
                send2[ph, :, cols] = first.astype(BF16)
                direct[ph, 0, :, cols] = second[half:].astype(BF16)
                sums[ph, 0, :, cols] = second[0:half]
            else:
                direct[ph, 1, :, cols] = first[0:half].astype(BF16)
                sums[ph, 1, :, cols] = first[half:]
                sums[ph, 2, :, cols] = second[0:half]
                sums[ph, 3, :, cols] = second[half:]
        if pair == 0:
            relay_sums[ph] = [
                remote(send2.at[ph, pl.ds(0, half)], relay_in.at[ph, 0], right),
                remote(send2.at[ph, pl.ds(half, half)], relay_in.at[ph, 1], left),
            ]
            final_sums[ph] = [remote(direct.at[ph, 0], final_in.at[ph, 0, 1], right)]
        else:
            final_sums[ph].append(remote(direct.at[ph, 1], final_in.at[ph, 1, 0], left))

    def wait_partner(ph):
        if ph == 0:
            phid_copy.wait_recv()
        for si in range(Z):
            prow_copies[ph, si].wait_recv()

    def pass_sums(ph):
        for side in range(2):
            relay_sums[ph][side].wait_recv()
            relayed[ph, side] = (sums[ph, side] + relay_in[ph, side].astype(F32)).astype(BF16)
            final_sums[ph].append(
                remote(relayed.at[ph, side], final_in.at[ph, side, side], (right, left)[side]))

    gd_copies = []

    def finish_sums(ph):
        for copy in final_sums[ph]:
            copy.wait_recv()
        for part in range(2):
            gdb[ph, pl.ds(part * half, half)] = (
                sums[ph, 2 + part] + final_in[ph, 0, part].astype(F32)
                + final_in[ph, 1, part].astype(F32)
            ).astype(BF16)
        gd_copies.append(local(gdb.at[ph], gd.at[pl.ds(ph * sub, sub)]))

    for direction in range(2):
        forward_tab(direction, 0)
    for g in range(2):
        for direction in range(2):
            forward(direction, 0, g)
    phid_copy = remote(hid_in, phid, partner)

    arrivals = []
    for ph in range(PHASES):
        arrivals += [(8 * ph, ph, (0,))]
        arrivals += [(8 * ph + 2 * d, ph, (d, 4 + d)) for d in (1, 2, 3)]
        arrivals += [(8 * ph + 7, ph, (4,))]
    todo = {}
    for ev, ph, sis in arrivals:
        todo.setdefault(ev + ARRIVE_LAG, []).append((ph, sis))

    for ev in range(8 * PHASES):
        ph, i = ev // 8, ev % 8
        g0 = 2 * ph
        if i == 0:
            unit(ph, ev, g0, own.at[g0], 0)
            unit(ph, ev, g0 + 1, own.at[g0 + 1], 0)
        elif i < 7:
            d, cc = (i + 1) // 2, (i + 1) % 2
            g = g0 + cc
            if ph == 0 and cc == 0:
                for direction in range(2):
                    tab_copies[direction, d].wait_recv()
                    if d < 4 - direction:
                        forward_tab(direction, d)
            for direction in range(2):
                z_copies[direction, d, g].wait_recv()
                if d < 3 or cc == direction:
                    forward(direction, d, g)
            if i in (5, 6) and ph + 1 < PHASES:
                for load in own_loads[g + 2]:
                    load.wait()
                for direction in range(2):
                    forward(direction, 0, g + 2)
            for direction in range(2):
                si = tab_index(direction, d)
                if ph == 0 and cc == 0:
                    make_pick(si)
                unit(ph, ev, g, zbuf.at[direction, d - 1, g], si)
        else:
            if ph == 0:
                tab_copies[0, 4].wait_recv()
                make_pick(4)
            for direction in range(2):
                z_copies[direction, 4, g0 + direction].wait_recv()
                unit(ph, ev, g0 + direction, zbuf.at[direction, 3, g0 + direction], 4)
        for ready_ph, sis in todo.pop(ev, []):
            arrive(ready_ph, sis)
            project(ready_ph, sis)
        if ph > 0 and i == 4:
            wait_partner(ph - 1)
            weight_grad(ph - 1, 0)
        if ph > 0 and i == 5:
            weight_grad(ph - 1, 1)
        if ph > 0 and i == 7:
            pass_sums(ph - 1)

    rest = [item for ev in sorted(todo) for item in todo[ev]]
    for ready_ph, sis in rest:
        arrive(ready_ph, sis)
    for ready_ph, sis in rest[:-1]:
        project(ready_ph, sis)
    wait_partner(PHASES - 1)
    weight_grad(PHASES - 1, 0)
    weight_grad(PHASES - 1, 1)
    project(*rest[-1])

    sgy[y] = sg[...]
    back = [remote(sg, sgy.at[y], peer) for peer in (side_a, side_b, side_far)]
    finish_sums(0)
    pass_sums(PHASES - 1)
    for copy in back:
        copy.wait_recv()
    for zz in range(Z):
        for yy in range(Y):
            sgu[zz, yy:yy + 1] = sgy[yy, zz:zz + 1]
        sgu[zz, Y:8] = jnp.zeros((8 - Y, tokens), F32)
    sgz[z] = sgu[z]
    back = [remote(sgu.at[(z + d) % Z], sgz.at[z], at_ex((z + d) % Z, y)) for d in range(1, Z)]

    row_id = lax.broadcasted_iota(jnp.int32, (8 * Z, tokens), 0)
    expert_of_row = jnp.where(row_id % 8 < Y, row_id // 8 * Y + row_id % 8, -1).astype(F32)
    marks = jnp.zeros((8 * Z, tokens), F32)
    for k in range(picks):
        marks = marks + jnp.where(expert_of_row == ids_f[k:k + 1], 1.0, 0.0)
    rank = jnp.dot(marks.astype(BF16), before, preferred_element_type=F32)
    slot = jnp.where(marks > 0.5, rank, -1.0)
    for copy in back:
        copy.wait_recv()
    table = sgz[...].reshape(8 * Z, tokens)
    values = jnp.zeros((8 * Z, cap), F32)
    for yy in range(Y):
        values = jnp.where(y == yy, table[:, yy * cap:(yy + 1) * cap], values)
    found = jnp.zeros((8 * Z, tokens), F32)
    for cc in range(cap):
        found = jnp.where(slot == float(cc), values[:, cc:cc + 1], found)
    for k in range(picks):
        gp[k:k + 1, :] = jnp.sum(
            jnp.where(expert_of_row == ids_f[k:k + 1], found, 0.0), axis=0, keepdims=True
        ) / comb_f[k:k + 1]

    finish_sums(PHASES - 1)
    for copy in started:
        copy.wait_send()
    for copy in gh_copies + gd_copies:
        copy.wait()


def body(out_grad, combine, expert_ids, hidden, w_down):
    tokens, picks = expert_ids.shape
    width = out_grad.shape[1]
    cap, inner = hidden.shape[2], hidden.shape[3]
    groups = 2 * PHASES
    gcols = width // groups
    sub = gcols // X
    flat = (Z, Y * cap)
    vmem = lambda shape, kind=BF16: pltpu.VMEM(shape, kind)
    in_place = lambda a: pltpu.with_memory_space_constraint(a, pltpu.HBM)
    anywhere = pl.BlockSpec(memory_space=pl.ANY)
    in_hbm = pl.BlockSpec(memory_space=pltpu.HBM)
    in_vmem = pl.BlockSpec(memory_space=pltpu.VMEM)
    grad_hidden, grad_down, grad_probs = pl.pallas_call(
        kernel,
        out_shape=(
            jax.ShapeDtypeStruct(flat + (inner,), BF16),
            jax.ShapeDtypeStruct((PHASES * sub, inner), BF16),
            jax.ShapeDtypeStruct((picks, tokens), F32),
        ),
        in_specs=[in_hbm, in_vmem, in_vmem, in_hbm, in_hbm],
        out_specs=(anywhere, anywhere, in_vmem),
        scratch_shapes=[
            vmem((groups, tokens, gcols)),
            vmem((2, 4, groups, tokens, gcols)),
            vmem((Z, 16, tokens)),
            vmem((Z, tokens, tokens)),
            vmem((16 * PHASES, 3, cap, gcols)),
            vmem((groups,) + flat + (gcols,)),
            vmem((PHASES,) + flat + (gcols,)),
            vmem(flat + (inner,)),
            vmem(flat + (inner,)),
            vmem((PHASES, 2 * gcols, inner)),
            vmem(flat + (inner,), F32),
            vmem(flat + (inner,)),
            vmem((PHASES, 4, sub // 2, inner), F32),
            vmem((PHASES, sub, inner)),
            vmem((PHASES, 2, sub // 2, inner)),
            vmem((PHASES, 2, sub // 2, inner)),
            vmem((PHASES, 2, sub // 2, inner)),
            vmem((PHASES, 2, 2, sub // 2, inner)),
            vmem((PHASES, sub, inner)),
            vmem((Z, tokens), F32),
            vmem((Y, Z, tokens), F32),
            vmem((Z, 8, tokens), F32),
            vmem((Z, 8, tokens), F32),
            pltpu.SemaphoreType.DMA((512,)),
        ],
        compiler_params=pltpu.CompilerParams(
            collective_id=0, has_side_effects=True, vmem_limit_bytes=46 * 2**20),
    )(
        in_place(out_grad), expert_ids.T, combine.T,
        in_place(hidden.reshape(flat + (inner,))), in_place(w_down[0]),
    )
    return (
        grad_hidden.reshape(hidden.shape),
        grad_down[None],
        grad_probs.T,
    )


def solution(mesh):
    in_specs = (
        P(("dp", "expert"), None),
        P(("dp", "expert"), None),
        P(("dp", "expert"), None),
        P("expert", "dp", None, None),
        P("expert", None, None),
    )
    out_specs = (P("expert", "dp", None, None), P("expert", "dp", None), P(("dp", "expert"), None))
    return jax.shard_map(body, mesh=mesh, in_specs=in_specs, out_specs=out_specs, check_vma=False)
```

```python
import functools

import jax
import jax.numpy as jnp
from jax import lax
from jax.experimental import pallas as pl
from jax.experimental.pallas import tpu as pltpu
from jax.sharding import PartitionSpec as P

MESH = pl.DeviceIdType.MESH
F32 = jnp.float32
BF16 = jnp.bfloat16
X, Y, Z = 4, 4, 8
PHASES = 2
ARRIVE_LAG = 4


def column_chunks(width):
    step = 512
    return [(at, min(step, width - at)) for at in range(0, width, step)]


def kernel(
    tok, ids_in, comb_in, hid_in, w_in, gh, gd, gp,
    ids, comb, own, zbuf, tab, pick, sel, rows, prow, hid, phid, wv, acc, ghb,
    sums, send2, direct, relayed, relay_in, final_in, gdb, sg, sgy, sgu, sgz,
    sems,
):
    tokens, group_cols = own.shape[1:]
    sub = group_cols // X
    cap = tokens // Y
    inner = hid.shape[-1]
    chunks = column_chunks(inner)
    dp, ex = lax.axis_index("dp"), lax.axis_index("expert")
    x, core = dp // 2, dp % 2
    z, y = ex // Y, ex % Y
    y_a, y_b, y_far = y + 1 - 2 * (y % 2), Y - 1 - y, (y + 2) % Y

    def at_ex(zz, yy):
        return {"expert": zz * Y + yy}

    def at_dp(xx, cc):
        return {"dp": xx * 2 + cc}

    up, down = at_ex((z + 1) % Z, y), at_ex((z + Z - 1) % Z, y)
    side_a, side_b, side_far = at_ex(z, y_a), at_ex(z, y_b), at_ex(z, y_far)
    right, left = at_dp((x + 1) % X, core), at_dp((x + X - 1) % X, core)
    partner = at_dp(x, 1 - core)

    taken = [0]
    started = []

    def sem():
        taken[0] += 1
        return sems.at[taken[0] - 1]

    def local(src, dst):
        copy = pltpu.make_async_copy(src, dst, sem())
        copy.start()
        return copy

    def remote(src, dst, device):
        copy = pltpu.make_async_remote_copy(
            src_ref=src, dst_ref=dst, send_sem=sem(), recv_sem=sem(),
            device_id=device, device_id_type=MESH,
        )
        copy.start()
        started.append(copy)
        return copy

    table_loads = [local(ids_in, ids), local(comb_in, comb)]
    own_loads = []
    for g in range(2 * PHASES):
        ph, cc = g // 2, g % 2
        own_loads.append([
            local(tok.at[:, pl.ds(q * 2 * 256 + cc * 256 + ph * sub, sub)],
                  own.at[g, :, pl.ds(q * sub, sub)])
            for q in range(X)
        ])
    hid_load = local(hid_in, hid)
    w_loads = []
    for ph in range(PHASES):
        for cc in range(2):
            for q in range(X):
                w_loads.append(local(
                    w_in.at[pl.ds(q * 512 + cc * 256 + ph * sub, sub)],
                    wv.at[ph, pl.ds(cc * group_cols + q * sub, sub)]))

    barrier = pltpu.get_barrier_semaphore()
    peers = [up, down, side_a, side_b, side_far, right, left, partner]
    for peer in peers:
        pl.semaphore_signal(barrier, inc=1, device_id=peer, device_id_type=MESH)

    for load in table_loads:
        load.wait()
    ids_f = ids[...].astype(F32)
    comb_f = comb[...].astype(F32)
    picks = ids_f.shape[0]
    pad = 8 - picks
    tab[0] = jnp.concatenate([
        ids_f, jnp.full((pad, tokens), -1.0, F32), comb_f, jnp.zeros((pad, tokens), F32)
    ], axis=0).astype(BF16)
    before = (
        lax.broadcasted_iota(jnp.int32, (tokens, tokens), 0)
        < lax.broadcasted_iota(jnp.int32, (tokens, tokens), 1)
    ).astype(F32).astype(BF16)
    slot_of_row = lax.broadcasted_iota(jnp.int32, (cap, tokens), 0).astype(F32)

    def make_pick(si):
        table = tab[si].astype(F32)
        named, weight = table[0:8], table[8:16]
        chosen, probs = [], []
        for yy in (y_a, y_far, y_b, y):
            hit = named == (z * Y + yy).astype(F32)
            chosen.append(jnp.sum(jnp.where(hit, 1.0, 0.0), axis=0, keepdims=True))
            probs.append(jnp.sum(jnp.where(hit, weight, 0.0), axis=0, keepdims=True))
        marks = jnp.concatenate(chosen + [jnp.zeros((4, tokens), F32)], axis=0)
        rank = jnp.dot(marks.astype(BF16), before, preferred_element_type=F32)
        blocks = []
        for b in range(4):
            slot = jnp.where(chosen[b] > 0.5, rank[b:b + 1], -1.0)
            blocks.append(jnp.where(slot_of_row == slot, probs[b], 0.0))
        pick[si] = jnp.concatenate(blocks, axis=0).astype(BF16)

    make_pick(0)
    for load in own_loads[0] + own_loads[1]:
        load.wait()
    pl.semaphore_wait(barrier, len(peers))

    def source_z(si):
        return (z + (Z - si if si < 5 else si - 4)) % Z

    z_copies, tab_copies = {}, {}

    def token_block(direction, d, g):
        return own.at[g] if d == 0 else zbuf.at[direction, d - 1, g]

    def forward(direction, d, g):
        z_copies[direction, d + 1, g] = remote(
            token_block(direction, d, g), zbuf.at[direction, d, g], (up, down)[direction])

    def tab_index(direction, d):
        return 0 if d == 0 else d + 4 * direction

    def forward_tab(direction, d):
        tab_copies[direction, d + 1] = remote(
            tab.at[tab_index(direction, d)], tab.at[tab_index(direction, d + 1)],
            (up, down)[direction])

    y_copies, events = {}, {}

    def unit(ph, ev, g, src, si):
        u = 2 * ev + len(events.setdefault(ev, []))
        zs = source_z(si)
        block = jnp.dot(pick[si], src[...], preferred_element_type=F32).astype(BF16)
        for b in range(3):
            sel[u, b] = block[b * cap:(b + 1) * cap]
        mine = pl.ds(pl.multiple_of(y * cap, cap), cap)
        rows[g, zs, mine] = block[3 * cap:]
        y_copies.setdefault((ph, si), []).extend([
            remote(sel.at[u, b], rows.at[g, zs, mine], peer)
            for b, peer in ((1, side_far), (0, side_a), (2, side_b))
        ])
        events[ev].append(u)

    prow_copies = {}

    def arrive(ph, sis):
        for si in sis:
            for copy in y_copies[ph, si]:
                copy.wait_recv()
            zs = source_z(si)
            prow_copies[ph, si] = remote(
                rows.at[2 * ph + 1 - core, zs], prow.at[ph, zs], partner)

    eye = (
        lax.broadcasted_iota(jnp.int32, (tokens, tokens), 0)
        == lax.broadcasted_iota(jnp.int32, (tokens, tokens), 1)
    )
    gh_copies = []
    w_waited = [False]

    def project(ph, sis):
        if not w_waited[0]:
            w_waited[0] = True
            hid_load.wait()
            for load in w_loads:
                load.wait()
        places = [source_z(si) for si in sis]
        halves = [
            jnp.concatenate([rows[2 * ph + cc, zs] for zs in places], axis=0) for cc in range(2)
        ]
        totals = [jnp.zeros((tokens, 1), F32) for _ in sis]
        for at, width in chunks:
            cols = pl.ds(at, width)
            value = jnp.dot(
                halves[0], wv[ph, 0:group_cols, cols], preferred_element_type=F32
            ) + jnp.dot(
                halves[1], wv[ph, group_cols:2 * group_cols, cols], preferred_element_type=F32)
            for n, zs in enumerate(places):
                part = value[n * tokens:(n + 1) * tokens]
                if ph > 0:
                    part = part + acc[zs, :, cols]
                if ph < PHASES - 1:
                    acc[zs, :, cols] = part
                else:
                    ghb[zs, :, cols] = part.astype(BF16)
                    totals[n] = totals[n] + jnp.sum(
                        part * hid[zs, :, cols].astype(F32), axis=1, keepdims=True)
        if ph == PHASES - 1:
            for n, zs in enumerate(places):
                gh_copies.append(local(ghb.at[zs], gh.at[zs]))
                sg[pl.ds(zs, 1), :] = jnp.sum(
                    jnp.where(eye, totals[n], 0.0), axis=0, keepdims=True)

    slices = [(x + 2) % X, (x + 1) % X, (x + X - 1) % X, x]
    half = sub // 2
    relay_sums, final_sums = {}, {}

    def weight_grad(ph, pair):
        lanes = [pl.ds(pl.multiple_of(q * sub, sub), sub) for q in slices[2 * pair:2 * pair + 2]]
        flat = Z * tokens
        mine = jnp.concatenate(
            [rows[2 * ph + core, :, :, q].reshape(flat, sub) for q in lanes], axis=1)
        others = jnp.concatenate(
            [prow[ph, :, :, q].reshape(flat, sub) for q in lanes], axis=1)
        contract = (((0,), (0,)), ((), ()))
        for at, width in chunks:
            cols = pl.ds(at, width)
            value = lax.dot_general(
                mine, hid[:, :, cols].reshape(flat, width), contract, preferred_element_type=F32
            ) + lax.dot_general(
                others, phid[:, :, cols].reshape(flat, width), contract,
                preferred_element_type=F32)
            first, second = value[0:sub], value[sub:2 * sub]
            if pair == 0:
                send2[ph, :, cols] = first.astype(BF16)
                direct[ph, 0, :, cols] = second[half:].astype(BF16)
                sums[ph, 0, :, cols] = second[0:half]
            else:
                direct[ph, 1, :, cols] = first[0:half].astype(BF16)
                sums[ph, 1, :, cols] = first[half:]
                sums[ph, 2, :, cols] = second[0:half]
                sums[ph, 3, :, cols] = second[half:]
        if pair == 0:
            relay_sums[ph] = [
                remote(send2.at[ph, pl.ds(0, half)], relay_in.at[ph, 0], right),
                remote(send2.at[ph, pl.ds(half, half)], relay_in.at[ph, 1], left),
            ]
            final_sums[ph] = [remote(direct.at[ph, 0], final_in.at[ph, 0, 1], right)]
        else:
            final_sums[ph].append(remote(direct.at[ph, 1], final_in.at[ph, 1, 0], left))

    def wait_partner(ph):
        if ph == 0:
            phid_copy.wait_recv()
        for si in range(Z):
            prow_copies[ph, si].wait_recv()

    def pass_sums(ph):
        for side in range(2):
            relay_sums[ph][side].wait_recv()
            relayed[ph, side] = (sums[ph, side] + relay_in[ph, side].astype(F32)).astype(BF16)
            final_sums[ph].append(
                remote(relayed.at[ph, side], final_in.at[ph, side, side], (right, left)[side]))

    gd_copies = []

    def finish_sums(ph):
        for copy in final_sums[ph]:
            copy.wait_recv()
        for part in range(2):
            gdb[ph, pl.ds(part * half, half)] = (
                sums[ph, 2 + part] + final_in[ph, 0, part].astype(F32)
                + final_in[ph, 1, part].astype(F32)
            ).astype(BF16)
        gd_copies.append(local(gdb.at[ph], gd.at[pl.ds(ph * sub, sub)]))

    for direction in range(2):
        forward_tab(direction, 0)
    for g in range(2):
        for direction in range(2):
            forward(direction, 0, g)
    phid_copy = remote(hid_in, phid, partner)

    def own_units(ph):
        for g in (2 * ph, 2 * ph + 1):
            unit(ph, 8 * ph, g, own.at[g], 0)

    arrivals = []
    for ph in range(PHASES):
        arrivals += [(8 * ph, ph, (0,))]
        arrivals += [(8 * ph + 2 * d, ph, (d, 4 + d)) for d in (1, 2, 3)]
        arrivals += [(8 * ph + 7, ph, (4,))]
    todo = {}
    for ev, ph, sis in arrivals:
        todo.setdefault(ev + ARRIVE_LAG, []).append((ph, sis))

    for ev in range(8 * PHASES):
        ph, i = ev // 8, ev % 8
        g0 = 2 * ph
        if i == 0:
            if ph == 0:
                own_units(0)
                for load in own_loads[2] + own_loads[3]:
                    load.wait()
                own_units(1)
        elif i < 7:
            d, cc = (i + 1) // 2, (i + 1) % 2
            g = g0 + cc
            if ph == 0 and cc == 0:
                for direction in range(2):
                    tab_copies[direction, d].wait_recv()
                    if d < 4 - direction:
                        forward_tab(direction, d)
            for direction in range(2):
                z_copies[direction, d, g].wait_recv()
                if d < 3 or cc == direction:
                    forward(direction, d, g)
            if i in (5, 6) and ph + 1 < PHASES:
                for direction in range(2):
                    forward(direction, 0, g + 2)
            for direction in range(2):
                si = tab_index(direction, d)
                if ph == 0 and cc == 0:
                    make_pick(si)
                unit(ph, ev, g, zbuf.at[direction, d - 1, g], si)
        else:
            if ph == 0:
                tab_copies[0, 4].wait_recv()
                make_pick(4)
            for direction in range(2):
                z_copies[direction, 4, g0 + direction].wait_recv()
                unit(ph, ev, g0 + direction, zbuf.at[direction, 3, g0 + direction], 4)
        for ready_ph, sis in todo.pop(ev, []):
            arrive(ready_ph, sis)
            project(ready_ph, sis)
        if ph > 0 and i == 4:
            wait_partner(ph - 1)
            weight_grad(ph - 1, 0)
        if ph > 0 and i == 5:
            weight_grad(ph - 1, 1)
        if ph > 0 and i == 7:
            pass_sums(ph - 1)

    rest = [item for ev in sorted(todo) for item in todo[ev]]
    for ready_ph, sis in rest:
        arrive(ready_ph, sis)
    for ready_ph, sis in rest[:-1]:
        project(ready_ph, sis)
    wait_partner(PHASES - 1)
    weight_grad(PHASES - 1, 0)
    weight_grad(PHASES - 1, 1)
    project(*rest[-1])

    sgy[y] = sg[...]
    back = [remote(sg, sgy.at[y], peer) for peer in (side_a, side_b, side_far)]
    finish_sums(0)
    pass_sums(PHASES - 1)
    for copy in back:
        copy.wait_recv()
    for zz in range(Z):
        for yy in range(Y):
            sgu[zz, yy:yy + 1] = sgy[yy, zz:zz + 1]
        sgu[zz, Y:8] = jnp.zeros((8 - Y, tokens), F32)
    sgz[z] = sgu[z]
    back = [remote(sgu.at[(z + d) % Z], sgz.at[z], at_ex((z + d) % Z, y)) for d in range(1, Z)]

    row_id = lax.broadcasted_iota(jnp.int32, (8 * Z, tokens), 0)
    expert_of_row = jnp.where(row_id % 8 < Y, row_id // 8 * Y + row_id % 8, -1).astype(F32)
    marks = jnp.zeros((8 * Z, tokens), F32)
    for k in range(picks):
        marks = marks + jnp.where(expert_of_row == ids_f[k:k + 1], 1.0, 0.0)
    rank = jnp.dot(marks.astype(BF16), before, preferred_element_type=F32)
    slot = jnp.where(marks > 0.5, rank, -1.0)
    for copy in back:
        copy.wait_recv()
    table = sgz[...].reshape(8 * Z, tokens)
    values = jnp.zeros((8 * Z, cap), F32)
    for yy in range(Y):
        values = jnp.where(y == yy, table[:, yy * cap:(yy + 1) * cap], values)
    found = jnp.zeros((8 * Z, tokens), F32)
    for cc in range(cap):
        found = jnp.where(slot == float(cc), values[:, cc:cc + 1], found)
    for k in range(picks):
        gp[k:k + 1, :] = jnp.sum(
            jnp.where(expert_of_row == ids_f[k:k + 1], found, 0.0), axis=0, keepdims=True
        ) / comb_f[k:k + 1]

    finish_sums(PHASES - 1)
    for copy in started:
        copy.wait_send()
    for copy in gh_copies + gd_copies:
        copy.wait()


def body(out_grad, combine, expert_ids, hidden, w_down):
    tokens, picks = expert_ids.shape
    width = out_grad.shape[1]
    cap, inner = hidden.shape[2], hidden.shape[3]
    groups = 2 * PHASES
    gcols = width // groups
    sub = gcols // X
    flat = (Z, Y * cap)
    vmem = lambda shape, kind=BF16: pltpu.VMEM(shape, kind)
    in_place = lambda a: pltpu.with_memory_space_constraint(a, pltpu.HBM)
    anywhere = pl.BlockSpec(memory_space=pl.ANY)
    in_hbm = pl.BlockSpec(memory_space=pltpu.HBM)
    in_vmem = pl.BlockSpec(memory_space=pltpu.VMEM)
    grad_hidden, grad_down, grad_probs = pl.pallas_call(
        kernel,
        out_shape=(
            jax.ShapeDtypeStruct(flat + (inner,), BF16),
            jax.ShapeDtypeStruct((PHASES * sub, inner), BF16),
            jax.ShapeDtypeStruct((picks, tokens), F32),
        ),
        in_specs=[in_hbm] * 5,
        out_specs=(anywhere, anywhere, in_vmem),
        scratch_shapes=[
            vmem((picks, tokens), jnp.int32),
            vmem((picks, tokens)),
            vmem((groups, tokens, gcols)),
            vmem((2, 4, groups, tokens, gcols)),
            vmem((Z, 16, tokens)),
            vmem((Z, tokens, tokens)),
            vmem((16 * PHASES, 3, cap, gcols)),
            vmem((groups,) + flat + (gcols,)),
            vmem((PHASES,) + flat + (gcols,)),
            vmem(flat + (inner,)),
            vmem(flat + (inner,)),
            vmem((PHASES, 2 * gcols, inner)),
            vmem(flat + (inner,), F32),
            vmem(flat + (inner,)),
            vmem((PHASES, 4, sub // 2, inner), F32),
            vmem((PHASES, sub, inner)),
            vmem((PHASES, 2, sub // 2, inner)),
            vmem((PHASES, 2, sub // 2, inner)),
            vmem((PHASES, 2, sub // 2, inner)),
            vmem((PHASES, 2, 2, sub // 2, inner)),
            vmem((PHASES, sub, inner)),
            vmem((Z, tokens), F32),
            vmem((Y, Z, tokens), F32),
            vmem((Z, 8, tokens), F32),
            vmem((Z, 8, tokens), F32),
            pltpu.SemaphoreType.DMA((512,)),
        ],
        compiler_params=pltpu.CompilerParams(
            collective_id=0, has_side_effects=True, vmem_limit_bytes=46 * 2**20),
    )(
        in_place(out_grad), in_place(expert_ids.T), in_place(combine.T),
        in_place(hidden.reshape(flat + (inner,))), in_place(w_down[0]),
    )
    return (
        grad_hidden.reshape(hidden.shape),
        grad_down[None],
        grad_probs.T,
    )


def solution(mesh):
    in_specs = (
        P(("dp", "expert"), None),
        P(("dp", "expert"), None),
        P(("dp", "expert"), None),
        P("expert", "dp", None, None),
        P("expert", None, None),
    )
    out_specs = (P("expert", "dp", None, None), P("expert", "dp", None), P(("dp", "expert"), None))
    return jax.shard_map(body, mesh=mesh, in_specs=in_specs, out_specs=out_specs, check_vma=False)
```

```python
import functools

import jax
import jax.numpy as jnp
from jax import lax
from jax.experimental import pallas as pl
from jax.experimental.pallas import tpu as pltpu
from jax.sharding import PartitionSpec as P

MESH = pl.DeviceIdType.MESH
F32 = jnp.float32
BF16 = jnp.bfloat16
X, Y, Z = 4, 4, 8
PHASES = 2
ARRIVE_LAG = 4


def column_chunks(width):
    step = 512
    return [(at, min(step, width - at)) for at in range(0, width, step)]


def kernel(
    tok, ids_in, comb_in, hid_in, w_in, gh, gd, gp,
    ids, comb, own, zbuf, tab, pick, sel, rows, prow, hid, phid, wv, acc, ghb,
    sums, send2, direct, relayed, relay_in, final_in, gdb, sg, sgy, sgu, sgz,
    sems,
):
    tokens, group_cols = own.shape[1:]
    sub = group_cols // X
    cap = tokens // Y
    inner = hid.shape[-1]
    chunks = column_chunks(inner)
    dp, ex = lax.axis_index("dp"), lax.axis_index("expert")
    x, core = dp // 2, dp % 2
    z, y = ex // Y, ex % Y
    y_a, y_b, y_far = y + 1 - 2 * (y % 2), Y - 1 - y, (y + 2) % Y

    def at_ex(zz, yy):
        return {"expert": zz * Y + yy}

    def at_dp(xx, cc):
        return {"dp": xx * 2 + cc}

    up, down = at_ex((z + 1) % Z, y), at_ex((z + Z - 1) % Z, y)
    side_a, side_b, side_far = at_ex(z, y_a), at_ex(z, y_b), at_ex(z, y_far)
    right, left = at_dp((x + 1) % X, core), at_dp((x + X - 1) % X, core)
    partner = at_dp(x, 1 - core)

    taken = [0]
    started = []

    def sem():
        taken[0] += 1
        return sems.at[taken[0] - 1]

    def local(src, dst):
        copy = pltpu.make_async_copy(src, dst, sem())
        copy.start()
        return copy

    def remote(src, dst, device):
        copy = pltpu.make_async_remote_copy(
            src_ref=src, dst_ref=dst, send_sem=sem(), recv_sem=sem(),
            device_id=device, device_id_type=MESH,
        )
        copy.start()
        started.append(copy)
        return copy

    table_loads = [local(ids_in, ids), local(comb_in, comb)]
    own_loads = []
    for g in range(2 * PHASES):
        ph, cc = g // 2, g % 2
        own_loads.append([
            local(tok.at[:, pl.ds(q * 2 * 256 + cc * 256 + ph * sub, sub)],
                  own.at[g, :, pl.ds(q * sub, sub)])
            for q in range(X)
        ])
    hid_load = local(hid_in, hid)
    w_loads = []
    for ph in range(PHASES):
        for cc in range(2):
            for q in range(X):
                w_loads.append(local(
                    w_in.at[pl.ds(q * 512 + cc * 256 + ph * sub, sub)],
                    wv.at[ph, pl.ds(cc * group_cols + q * sub, sub)]))

    barrier = pltpu.get_barrier_semaphore()
    peers = [up, down, side_a, side_b, side_far, right, left, partner]
    for peer in peers:
        pl.semaphore_signal(barrier, inc=1, device_id=peer, device_id_type=MESH)

    for load in table_loads:
        load.wait()
    ids_f = ids[...].astype(F32)
    comb_f = comb[...].astype(F32)
    picks = ids_f.shape[0]
    pad = 8 - picks
    tab[0] = jnp.concatenate([
        ids_f, jnp.full((pad, tokens), -1.0, F32), comb_f, jnp.zeros((pad, tokens), F32)
    ], axis=0).astype(BF16)
    before = (
        lax.broadcasted_iota(jnp.int32, (tokens, tokens), 0)
        < lax.broadcasted_iota(jnp.int32, (tokens, tokens), 1)
    ).astype(F32).astype(BF16)
    slot_of_row = lax.broadcasted_iota(jnp.int32, (cap, tokens), 0).astype(F32)

    def make_pick(si):
        table = tab[si].astype(F32)
        named, weight = table[0:8], table[8:16]
        chosen, probs = [], []
        for yy in (y_a, y_far, y_b, y):
            hit = named == (z * Y + yy).astype(F32)
            chosen.append(jnp.sum(jnp.where(hit, 1.0, 0.0), axis=0, keepdims=True))
            probs.append(jnp.sum(jnp.where(hit, weight, 0.0), axis=0, keepdims=True))
        marks = jnp.concatenate(chosen + [jnp.zeros((4, tokens), F32)], axis=0)
        rank = jnp.dot(marks.astype(BF16), before, preferred_element_type=F32)
        blocks = []
        for b in range(4):
            slot = jnp.where(chosen[b] > 0.5, rank[b:b + 1], -1.0)
            blocks.append(jnp.where(slot_of_row == slot, probs[b], 0.0))
        pick[si] = jnp.concatenate(blocks, axis=0).astype(BF16)

    make_pick(0)
    for load in own_loads[0] + own_loads[1]:
        load.wait()
    pl.semaphore_wait(barrier, len(peers))

    def source_z(si):
        return (z + (Z - si if si < 5 else si - 4)) % Z

    z_copies, tab_copies = {}, {}

    def token_block(direction, d, g):
        return own.at[g] if d == 0 else zbuf.at[direction, d - 1, g]

    def forward(direction, d, g):
        z_copies[direction, d + 1, g] = remote(
            token_block(direction, d, g), zbuf.at[direction, d, g], (up, down)[direction])

    def tab_index(direction, d):
        return 0 if d == 0 else d + 4 * direction

    def forward_tab(direction, d):
        tab_copies[direction, d + 1] = remote(
            tab.at[tab_index(direction, d)], tab.at[tab_index(direction, d + 1)],
            (up, down)[direction])

    y_copies, events = {}, {}

    def unit(ph, ev, g, src, si):
        u = 2 * ev + len(events.setdefault(ev, []))
        zs = source_z(si)
        block = jnp.dot(pick[si], src[...], preferred_element_type=F32).astype(BF16)
        for b in range(3):
            sel[u, b] = block[b * cap:(b + 1) * cap]
        mine = pl.ds(pl.multiple_of(y * cap, cap), cap)
        rows[g, zs, mine] = block[3 * cap:]
        y_copies.setdefault((ph, si), []).extend([
            remote(sel.at[u, b], rows.at[g, zs, mine], peer)
            for b, peer in ((1, side_far), (0, side_a), (2, side_b))
        ])
        events[ev].append(u)

    prow_copies = {}

    def arrive(ph, sis):
        for si in sis:
            for copy in y_copies[ph, si]:
                copy.wait_recv()
            zs = source_z(si)
            prow_copies[ph, si] = remote(
                rows.at[2 * ph + 1 - core, zs], prow.at[ph, zs], partner)

    eye = (
        lax.broadcasted_iota(jnp.int32, (tokens, tokens), 0)
        == lax.broadcasted_iota(jnp.int32, (tokens, tokens), 1)
    )
    gh_copies = []
    w_waited = [False]

    def project(ph, sis):
        if not w_waited[0]:
            w_waited[0] = True
            hid_load.wait()
            for load in w_loads:
                load.wait()
        places = [source_z(si) for si in sis]
        halves = [
            jnp.concatenate([rows[2 * ph + cc, zs] for zs in places], axis=0) for cc in range(2)
        ]
        totals = [jnp.zeros((tokens, 1), F32) for _ in sis]
        for at, width in chunks:
            cols = pl.ds(at, width)
            value = jnp.dot(
                halves[0], wv[ph, 0:group_cols, cols], preferred_element_type=F32
            ) + jnp.dot(
                halves[1], wv[ph, group_cols:2 * group_cols, cols], preferred_element_type=F32)
            for n, zs in enumerate(places):
                part = value[n * tokens:(n + 1) * tokens]
                if ph > 0:
                    part = part + acc[zs, :, cols]
                if ph < PHASES - 1:
                    acc[zs, :, cols] = part
                else:
                    ghb[zs, :, cols] = part.astype(BF16)
                    totals[n] = totals[n] + jnp.sum(
                        part * hid[zs, :, cols].astype(F32), axis=1, keepdims=True)
        if ph == PHASES - 1:
            for n, zs in enumerate(places):
                gh_copies.append(local(ghb.at[zs], gh.at[zs]))
                sg[pl.ds(zs, 1), :] = jnp.sum(
                    jnp.where(eye, totals[n], 0.0), axis=0, keepdims=True)

    slices = [(x + 2) % X, (x + 1) % X, (x + X - 1) % X, x]
    half = sub // 2
    relay_sums, final_sums = {}, {}

    def weight_grad(ph, pair):
        lanes = [pl.ds(pl.multiple_of(q * sub, sub), sub) for q in slices[2 * pair:2 * pair + 2]]
        flat = Z * tokens
        mine = jnp.concatenate(
            [rows[2 * ph + core, :, :, q].reshape(flat, sub) for q in lanes], axis=1)
        others = jnp.concatenate(
            [prow[ph, :, :, q].reshape(flat, sub) for q in lanes], axis=1)
        contract = (((0,), (0,)), ((), ()))
        for at, width in chunks:
            cols = pl.ds(at, width)
            value = lax.dot_general(
                mine, hid[:, :, cols].reshape(flat, width), contract, preferred_element_type=F32
            ) + lax.dot_general(
                others, phid[:, :, cols].reshape(flat, width), contract,
                preferred_element_type=F32)
            first, second = value[0:sub], value[sub:2 * sub]
            if pair == 0:
                send2[ph, :, cols] = first.astype(BF16)
                direct[ph, 0, :, cols] = second[half:].astype(BF16)
                sums[ph, 0, :, cols] = second[0:half]
            else:
                direct[ph, 1, :, cols] = first[0:half].astype(BF16)
                sums[ph, 1, :, cols] = first[half:]
                sums[ph, 2, :, cols] = second[0:half]
                sums[ph, 3, :, cols] = second[half:]
        if pair == 0:
            relay_sums[ph] = [
                remote(send2.at[ph, pl.ds(0, half)], relay_in.at[ph, 0], right),
                remote(send2.at[ph, pl.ds(half, half)], relay_in.at[ph, 1], left),
            ]
            final_sums[ph] = [remote(direct.at[ph, 0], final_in.at[ph, 0, 1], right)]
        else:
            final_sums[ph].append(remote(direct.at[ph, 1], final_in.at[ph, 1, 0], left))

    def wait_partner(ph):
        if ph == 0:
            phid_copy.wait_recv()
        for si in range(Z):
            prow_copies[ph, si].wait_recv()

    def pass_sums(ph):
        for side in range(2):
            relay_sums[ph][side].wait_recv()
            relayed[ph, side] = (sums[ph, side] + relay_in[ph, side].astype(F32)).astype(BF16)
            final_sums[ph].append(
                remote(relayed.at[ph, side], final_in.at[ph, side, side], (right, left)[side]))

    gd_copies = []

    def finish_sums(ph):
        for copy in final_sums[ph]:
            copy.wait_recv()
        for part in range(2):
            gdb[ph, pl.ds(part * half, half)] = (
                sums[ph, 2 + part] + final_in[ph, 0, part].astype(F32)
                + final_in[ph, 1, part].astype(F32)
            ).astype(BF16)
        gd_copies.append(local(gdb.at[ph], gd.at[pl.ds(ph * sub, sub)]))

    for direction in range(2):
        forward_tab(direction, 0)
    for g in range(2):
        for direction in range(2):
            forward(direction, 0, g)

    def own_units(ph):
        for g in (2 * ph, 2 * ph + 1):
            unit(ph, 8 * ph, g, own.at[g], 0)

    arrivals = []
    for ph in range(PHASES):
        arrivals += [(8 * ph, ph, (0,))]
        arrivals += [(8 * ph + 2 * d, ph, (d, 4 + d)) for d in (1, 2, 3)]
        arrivals += [(8 * ph + 7, ph, (4,))]
    todo = {}
    for ev, ph, sis in arrivals:
        todo.setdefault(ev + ARRIVE_LAG, []).append((ph, sis))

    for ev in range(8 * PHASES):
        ph, i = ev // 8, ev % 8
        if ev == 5:
            phid_copy = remote(hid_in, phid, partner)
        g0 = 2 * ph
        if i == 0:
            if ph == 0:
                own_units(0)
                for load in own_loads[2] + own_loads[3]:
                    load.wait()
                own_units(1)
        elif i < 7:
            d, cc = (i + 1) // 2, (i + 1) % 2
            g = g0 + cc
            if ph == 0 and cc == 0:
                for direction in range(2):
                    tab_copies[direction, d].wait_recv()
                    if d < 4 - direction:
                        forward_tab(direction, d)
            for direction in range(2):
                z_copies[direction, d, g].wait_recv()
                if d < 3 or cc == direction:
                    forward(direction, d, g)
            if i in (5, 6) and ph + 1 < PHASES:
                for direction in range(2):
                    forward(direction, 0, g + 2)
            for direction in range(2):
                si = tab_index(direction, d)
                if ph == 0 and cc == 0:
                    make_pick(si)
                unit(ph, ev, g, zbuf.at[direction, d - 1, g], si)
        else:
            if ph == 0:
                tab_copies[0, 4].wait_recv()
                make_pick(4)
            for direction in range(2):
                z_copies[direction, 4, g0 + direction].wait_recv()
                unit(ph, ev, g0 + direction, zbuf.at[direction, 3, g0 + direction], 4)
        for ready_ph, sis in todo.pop(ev, []):
            arrive(ready_ph, sis)
            project(ready_ph, sis)
        if ph > 0 and i == 4:
            wait_partner(ph - 1)
            weight_grad(ph - 1, 0)
        if ph > 0 and i == 5:
            weight_grad(ph - 1, 1)
        if ph > 0 and i == 7:
            pass_sums(ph - 1)

    rest = [item for ev in sorted(todo) for item in todo[ev]]
    for ready_ph, sis in rest:
        arrive(ready_ph, sis)
    for ready_ph, sis in rest[:-1]:
        project(ready_ph, sis)
    wait_partner(PHASES - 1)
    weight_grad(PHASES - 1, 0)
    weight_grad(PHASES - 1, 1)
    project(*rest[-1])

    sgy[y] = sg[...]
    back = [remote(sg, sgy.at[y], peer) for peer in (side_a, side_b, side_far)]
    finish_sums(0)
    for copy in back:
        copy.wait_recv()
    for zz in range(Z):
        for yy in range(Y):
            sgu[zz, yy:yy + 1] = sgy[yy, zz:zz + 1]
        sgu[zz, Y:8] = jnp.zeros((8 - Y, tokens), F32)
    sgz[z] = sgu[z]
    back = [remote(sgu.at[(z + d) % Z], sgz.at[z], at_ex((z + d) % Z, y)) for d in range(1, Z)]
    pass_sums(PHASES - 1)

    row_id = lax.broadcasted_iota(jnp.int32, (8 * Z, tokens), 0)
    expert_of_row = jnp.where(row_id % 8 < Y, row_id // 8 * Y + row_id % 8, -1).astype(F32)
    marks = jnp.zeros((8 * Z, tokens), F32)
    for k in range(picks):
        marks = marks + jnp.where(expert_of_row == ids_f[k:k + 1], 1.0, 0.0)
    rank = jnp.dot(marks.astype(BF16), before, preferred_element_type=F32)
    slot = jnp.where(marks > 0.5, rank, -1.0)
    for copy in back:
        copy.wait_recv()
    table = sgz[...].reshape(8 * Z, tokens)
    values = jnp.zeros((8 * Z, cap), F32)
    for yy in range(Y):
        values = jnp.where(y == yy, table[:, yy * cap:(yy + 1) * cap], values)
    found = jnp.zeros((8 * Z, tokens), F32)
    for cc in range(cap):
        found = jnp.where(slot == float(cc), values[:, cc:cc + 1], found)
    for k in range(picks):
        gp[k:k + 1, :] = jnp.sum(
            jnp.where(expert_of_row == ids_f[k:k + 1], found, 0.0), axis=0, keepdims=True
        ) / comb_f[k:k + 1]

    finish_sums(PHASES - 1)
    for copy in started:
        copy.wait_send()
    for copy in gh_copies + gd_copies:
        copy.wait()


def body(out_grad, combine, expert_ids, hidden, w_down):
    tokens, picks = expert_ids.shape
    width = out_grad.shape[1]
    cap, inner = hidden.shape[2], hidden.shape[3]
    groups = 2 * PHASES
    gcols = width // groups
    sub = gcols // X
    flat = (Z, Y * cap)
    vmem = lambda shape, kind=BF16: pltpu.VMEM(shape, kind)
    in_place = lambda a: pltpu.with_memory_space_constraint(a, pltpu.HBM)
    anywhere = pl.BlockSpec(memory_space=pl.ANY)
    in_hbm = pl.BlockSpec(memory_space=pltpu.HBM)
    in_vmem = pl.BlockSpec(memory_space=pltpu.VMEM)
    grad_hidden, grad_down, grad_probs = pl.pallas_call(
        kernel,
        out_shape=(
            jax.ShapeDtypeStruct(flat + (inner,), BF16),
            jax.ShapeDtypeStruct((PHASES * sub, inner), BF16),
            jax.ShapeDtypeStruct((picks, tokens), F32),
        ),
        in_specs=[in_hbm] * 5,
        out_specs=(anywhere, anywhere, in_vmem),
        scratch_shapes=[
            vmem((picks, tokens), jnp.int32),
            vmem((picks, tokens)),
            vmem((groups, tokens, gcols)),
            vmem((2, 4, groups, tokens, gcols)),
            vmem((Z, 16, tokens)),
            vmem((Z, tokens, tokens)),
            vmem((16 * PHASES, 3, cap, gcols)),
            vmem((groups,) + flat + (gcols,)),
            vmem((PHASES,) + flat + (gcols,)),
            vmem(flat + (inner,)),
            vmem(flat + (inner,)),
            vmem((PHASES, 2 * gcols, inner)),
            vmem(flat + (inner,), F32),
            vmem(flat + (inner,)),
            vmem((PHASES, 4, sub // 2, inner), F32),
            vmem((PHASES, sub, inner)),
            vmem((PHASES, 2, sub // 2, inner)),
            vmem((PHASES, 2, sub // 2, inner)),
            vmem((PHASES, 2, sub // 2, inner)),
            vmem((PHASES, 2, 2, sub // 2, inner)),
            vmem((PHASES, sub, inner)),
            vmem((Z, tokens), F32),
            vmem((Y, Z, tokens), F32),
            vmem((Z, 8, tokens), F32),
            vmem((Z, 8, tokens), F32),
            pltpu.SemaphoreType.DMA((512,)),
        ],
        compiler_params=pltpu.CompilerParams(
            collective_id=0, has_side_effects=True, vmem_limit_bytes=46 * 2**20),
    )(
        in_place(out_grad), in_place(expert_ids.T), in_place(combine.T),
        in_place(hidden.reshape(flat + (inner,))), in_place(w_down[0]),
    )
    return (
        grad_hidden.reshape(hidden.shape),
        grad_down[None],
        grad_probs.T,
    )


def solution(mesh):
    in_specs = (
        P(("dp", "expert"), None),
        P(("dp", "expert"), None),
        P(("dp", "expert"), None),
        P("expert", "dp", None, None),
        P("expert", None, None),
    )
    out_specs = (P("expert", "dp", None, None), P("expert", "dp", None), P(("dp", "expert"), None))
    return jax.shard_map(body, mesh=mesh, in_specs=in_specs, out_specs=out_specs, check_vma=False)
```
